32 devices in a mesh: band: 4 (over y, x), col: 8 (over z, core).
Axes of the slice: x: 2, y: 2, z: 4, core: 2. Of those that a mesh axis runs over, the one named last changes fastest.
Arguments:
- control: bfloat16 [4, 640, 320, 137], P('band', 'col'), may hold values from -6 to 6
- vertical_root: bfloat16 [3, 137, 128], replicated, may hold values from -0.5 to 0.5
- legendre: bfloat16 [320, 320, 320], P('col'), may hold values from -0.3125 to 0.3125
- band_filter: float32 [3, 320], replicated, may hold values from 0.3 to 1.7
- row_plan: int32 [4, 2], P('band'), may hold values from 0 to 16, as said below
- wave_order: int32 [320], replicated, may hold values from 0 to 319, each once
- lat_points: int32 [320], P('col'), may hold values from 16 to 640, as said below
- support: int32 [3, 2], replicated, may hold values from 0 to 320, as said below
Outputs:
- spectrum: float32 [320, 320, 2, 128], P('col', 'band')
The draws below stay inside these ranges and needn't reach their ends.
Inputs may be any that keep to these rules, and one draw needn't show every extreme that they name: `row_plan`: column 0 is the band of the row: 2 (coarsest) on max(1, 0) rows, 1 on max(1, 0) rows, 0 (finest) on the rest, rows drawn at random. Column 1 is the row's first output level; some row starts at 0 and some at 16. `lat_points`: counts rise with the distance from the nearest pole, apart from a jitter of up to 7 points between neighbouring latitudes; latitudes near the equator have all 640 points. `support`: row b is band b; band 0 ends at 320, band 2 starts at 0; every band's range is non-empty and the ranges of neighbouring bands intersect.
All inputs are finite; a program needn't handle non-finite values.
Results may differ from the reference program's by a relative error of at most 0.012.
Values may be sent and summed in bfloat16 or wider, within the bound.
A program may use at most 128 MiB of HBM per device.

```python
import math
import jax
import jax.numpy as jnp
from jax import lax

LON = 640
LAT = 320
M = 320
N = 320
LEV = 137
LVR = 112
SHIFT = 16
LEVW = 128
N_BAND = 4


def draw_row_plan(key, part):
    key_perm, key_start = jax.random.split(jax.random.fold_in(key, 11), 2)
    coarse = max(1, N_BAND // 16)
    middle = max(1, 3 * N_BAND // 16)
    shuffled = jax.random.permutation(key_perm, N_BAND)
    position = jnp.argsort(shuffled).astype(jnp.int32)
    band_column = jnp.where(position < coarse, 2, jnp.where(position < coarse + middle, 1, 0)).astype(jnp.int32)
    first_level = jax.random.randint(key_start, (N_BAND,), 0, SHIFT + 1, dtype=jnp.int32)
    first_level = jnp.where(position == 0, SHIFT, jnp.where(position == N_BAND - 1, 0, first_level)).astype(jnp.int32)
    return jnp.stack([band_column, first_level], axis=1).astype(jnp.int32)


def draw_lat_points(key, part):
    lat_axis = jnp.arange(LAT, dtype=jnp.int32)
    pole_dist = jnp.minimum(lat_axis, LAT - 1 - lat_axis)
    jitter = jax.random.randint(jax.random.fold_in(key, 23), (LAT,), 0, 8, dtype=jnp.int32)
    counts = 16 + 3 * LON * pole_dist // LAT + jitter
    return jnp.minimum(counts, LON).astype(jnp.int32)


def draw_support(key, part):
    keys = jax.random.split(jax.random.fold_in(key, 37), 4)
    fine_lo = jax.random.randint(keys[0], (), N // 8, N // 4 + 1, dtype=jnp.int32)
    mid_lo = jax.random.randint(keys[1], (), N // 16, N // 8 + 1, dtype=jnp.int32)
    mid_hi = jax.random.randint(keys[2], (), N // 2, 3 * N // 4 + 1, dtype=jnp.int32)
    coarse_hi = jax.random.randint(keys[3], (), N // 4, N // 2 + 1, dtype=jnp.int32)
    lows = jnp.stack([fine_lo, mid_lo, jnp.zeros((), jnp.int32)])
    highs = jnp.stack([jnp.full((), N, jnp.int32), mid_hi, coarse_hi])
    return jnp.stack([lows, highs], axis=1).astype(jnp.int32)


def levels(own_key, extent, shards, low, top_value):
    def one(dim, shards_of):
        draws = jax.random.uniform(jax.random.fold_in(jax.random.fold_in(own_key, 6), dim), (shards_of,), jnp.float32, low / len(shards), top_value / len(shards))
        return jnp.repeat(jnp.exp(draws), extent[dim] // shards_of).reshape((-1,) + (1,) * (len(extent) - dim - 1))

    factor_of = one(*shards[0])
    for cut in shards[1:]:
        factor_of = factor_of * one(*cut)
    return factor_of


def noise(own_key, extent, scale, limit, shards=(), held_as=jnp.bfloat16):
    factor_of = levels(own_key, extent, shards, -0.22, 0.18) if shards else 1.0
    entries = jax.random.normal(own_key, extent, jnp.float32) * scale * factor_of
    return jnp.minimum(jnp.maximum(entries, -limit), limit).astype(held_as)


def setup_inputs(seed: int = 0) -> dict:
    seeds = jax.random.split(jax.random.key(seed), 9)
    control = noise(seeds[0], (N_BAND, LON, LAT, LEV), 1.0, 6.0, ((0, 4), (1, 8)))
    vertical_root = noise(seeds[1], (3, LEV, LEVW), LEV ** -0.5, 0.5)
    legendre = noise(seeds[2], (M, LAT, N), LAT ** -0.5, 0.3125, ((0, 8),))
    band_filter = jnp.clip(jax.random.uniform(seeds[3], (3, N), jnp.float32, 0.3, 1.7), 0.3, 1.7)
    row_plan = draw_row_plan(jax.random.fold_in(seeds[8], 71), 0)
    wave_order = jax.random.permutation(seeds[5], M).astype(jnp.int32)
    lat_points = draw_lat_points(jax.random.fold_in(seeds[8], 71), 0)
    support = draw_support(jax.random.fold_in(seeds[8], 71), 0)
    return dict(control=control, vertical_root=vertical_root, legendre=legendre, band_filter=band_filter, row_plan=row_plan, wave_order=wave_order, lat_points=lat_points, support=support)


def dft_rows(points, wave_list, lon_count):
    lon_index = jnp.arange(lon_count, dtype=jnp.int32)[:, None]
    phase_step = wave_list[None, :] * lon_index % points
    angles = 2.0 * math.pi * phase_step.astype(jnp.float32) / points.astype(jnp.float32)
    live_mask = (lon_index < points).astype(jnp.float32) / jnp.sqrt(points.astype(jnp.float32))
    return (jnp.concatenate([jnp.cos(angles), -jnp.sin(angles)], axis=1) * live_mask).astype(jnp.bfloat16)

def reference(control, vertical_root, legendre, band_filter, row_plan, wave_order, lat_points, support):
    row_count, lon_count, lat_count, lev_count = control.shape
    mode_count = legendre.shape[0]
    degree_count = legendre.shape[2]
    degree = jnp.arange(degree_count, dtype=jnp.int32)
    triangle = (degree[None, :] >= wave_order[:, None]).astype(jnp.float32)
    legendre_f = legendre.astype(jnp.float32)

    def one_row(running, row_index):
        band_id = row_plan[row_index, 0]
        level_start = row_plan[row_index, 1]
        root_band = lax.dynamic_index_in_dim(vertical_root, band_id, 0, keepdims=False)
        root_block = lax.dynamic_slice_in_dim(root_band, level_start, LVR, 1)
        flat = lax.dynamic_index_in_dim(control, row_index, 0, keepdims=False).reshape(lon_count * lat_count, lev_count)
        grid_field = jnp.dot(flat, root_block, preferred_element_type=jnp.float32).astype(jnp.bfloat16)
        grid_field = grid_field.reshape(lon_count, lat_count, LVR)

        def one_lat(lat_index):
            weights = dft_rows(lat_points[lat_index], wave_order, lon_count)
            column = lax.dynamic_index_in_dim(grid_field, lat_index, 1, keepdims=False)
            return lax.dot_general(weights, column, (((0,), (0,)), ((), ())), preferred_element_type=jnp.float32).astype(jnp.bfloat16)
        fourier = lax.map(one_lat, jnp.arange(lat_count, dtype=jnp.int32)).reshape(lat_count, 2, mode_count, LVR)
        spectral = jnp.einsum('xpsl,sxn->snpl', fourier.astype(jnp.float32), legendre_f)
        bounds = lax.dynamic_index_in_dim(support, band_id, 0, keepdims=False)
        filter_row = lax.dynamic_index_in_dim(band_filter, band_id, 0, keepdims=False)
        window = filter_row * ((degree >= bounds[0]) & (degree < bounds[1])).astype(jnp.float32)
        contribution = (spectral * (triangle * window[None, :])[:, :, None, None]).astype(jnp.bfloat16)
        contribution = lax.optimization_barrier(contribution).astype(jnp.float32)
        placed = jnp.zeros((mode_count, degree_count, 2, LEVW), jnp.float32)
        placed = lax.dynamic_update_slice_in_dim(placed, contribution, level_start, 3)
        return (running + placed, None)
    initial = jnp.zeros((mode_count, degree_count, 2, LEVW), jnp.float32)
    summed, unused = lax.scan(one_row, initial, jnp.arange(row_count, dtype=jnp.int32))
    return summed
```

```python
import math

import jax
import jax.numpy as jnp
from jax import lax
from jax.experimental import pallas as pl
from jax.experimental.pallas import tpu as pltpu
from jax.sharding import PartitionSpec as P

LVR = 112
CHUNKS = 2


def weights_kernel(points_ref, wave_ref, part_ref, out_ref):
    count = jnp.full((1, 1), points_ref[pl.program_id(0)], jnp.int32).astype(jnp.float32)
    _, cols, lons = out_ref.shape
    tile = 8 if cols % 16 else 16
    lon = lax.broadcasted_iota(jnp.int32, (1, lons), 1).astype(jnp.float32)
    inverse = 1.0 / count
    scale = jnp.where(lon < count, lax.rsqrt(count), 0.0)

    def rows(k, carry):
        at = pl.ds(pl.multiple_of(k * tile, tile), tile)
        turns = (4.0 * wave_ref[at, :]) * lon
        quarter = jnp.round(turns * inverse)
        theta = (turns - quarter * count) * ((0.5 * math.pi) * inverse)
        square = theta * theta
        quadrant = quarter.astype(jnp.int32) + part_ref[at, :]
        odd = (quadrant & 1) == 1
        value = jnp.where(odd, 1.0 / 362880.0, 1.0 / 40320.0)
        value = value * square + jnp.where(odd, -1.0 / 5040.0, -1.0 / 720.0)
        value = value * square + jnp.where(odd, 1.0 / 120.0, 1.0 / 24.0)
        value = value * square + jnp.where(odd, -1.0 / 6.0, -0.5)
        value = value * square + 1.0
        value = value * jnp.where(odd, theta, 1.0)
        sign = jnp.where(((quadrant + 1) & 2) == 0, scale, -scale)
        out_ref[0, at, :] = (value * sign).astype(jnp.bfloat16)
        return carry

    lax.fori_loop(0, cols // tile, rows, 0)


def dft_weights(points, waves, lon_count):
    owners, slots = waves.shape
    lats = points.shape[0]
    cols = owners * 2 * slots
    shape = (owners, 2, slots)
    wave = jnp.broadcast_to(waves.astype(jnp.float32)[:, None], shape).reshape(cols, 1)
    part = jnp.broadcast_to(
        jnp.arange(2, dtype=jnp.int32)[None, :, None], shape
    ).reshape(cols, 1)
    return pl.pallas_call(
        weights_kernel,
        grid_spec=pltpu.PrefetchScalarGridSpec(
            num_scalar_prefetch=1,
            grid=(lats,),
            in_specs=[
                pl.BlockSpec((cols, 1), lambda i, p: (0, 0)),
                pl.BlockSpec((cols, 1), lambda i, p: (0, 0)),
            ],
            out_specs=pl.BlockSpec((1, cols, lon_count), lambda i, p: (i, 0, 0)),
        ),
        out_shape=jax.ShapeDtypeStruct((lats, cols, lon_count), jnp.bfloat16),
        cost_estimate=pl.CostEstimate(
            flops=25 * lats * cols * lon_count,
            bytes_accessed=2 * lats * cols * lon_count,
            transcendentals=0,
        ),
        name="weights",
    )(points, wave, part)


def dft_kernel(weight_ref, grid_ref, out_ref):
    lons = grid_ref.shape[0] * grid_ref.shape[2]
    column = grid_ref[:, 0].reshape(lons, grid_ref.shape[3])
    result = jnp.dot(weight_ref[0], column, preferred_element_type=jnp.float32)
    owners, _, rows, levels = out_ref.shape
    out_ref[:, 0] = result.astype(jnp.bfloat16).reshape(owners, rows, levels)


def dft(weights, grid_field, owners):
    lats, cols, lons = weights.shape
    ranks, _, lon_local, levels = grid_field.shape
    rows = cols // owners
    return pl.pallas_call(
        dft_kernel,
        grid=(lats,),
        in_specs=[
            pl.BlockSpec((1, cols, lons), lambda i: (i, 0, 0)),
            pl.BlockSpec((ranks, 1, lon_local, levels), lambda i: (0, i, 0, 0)),
        ],
        out_specs=pl.BlockSpec((owners, 1, rows, levels), lambda i: (0, i, 0, 0)),
        out_shape=jax.ShapeDtypeStruct((owners, lats, rows, levels), jnp.bfloat16),
        cost_estimate=pl.CostEstimate(
            flops=2 * lats * cols * lons * levels,
            bytes_accessed=2 * lats * (cols * lons + (cols + lons) * levels),
            transcendentals=0,
        ),
        name="dft",
    )(weights, grid_field)


def per_device(
    control, vertical_root, legendre, band_filter, row_plan, wave_order, lat_points, support
):
    owners = lax.axis_size("col")
    band_id = row_plan[0, 0]
    level_start = row_plan[0, 1]
    root_band = lax.dynamic_index_in_dim(vertical_root, band_id, 0, keepdims=False)
    level = jnp.arange(root_band.shape[1], dtype=jnp.int32)
    inside = (level >= level_start) & (level < level_start + LVR)
    root_block = jnp.where(inside[None, :], root_band, jnp.zeros_like(root_band))
    columns = control[0]
    lon_local, lat_count, _ = columns.shape
    rooted = jnp.einsum(
        "jik,kl->ijl", columns, root_block, preferred_element_type=jnp.float32
    ).astype(jnp.bfloat16)
    rooted = rooted.reshape(owners, lat_count // owners, lon_local, -1)
    grid_field = lax.all_to_all(rooted, "col", split_axis=0, concat_axis=0, tiled=True)
    lon_count = lon_local * owners
    lat_local = lat_count // owners

    slot_count = legendre.shape[0]
    degree_count = legendre.shape[2]
    step = slot_count // CHUNKS
    waves = wave_order.reshape(owners, CHUNKS, step)
    owned_waves = lax.dynamic_index_in_dim(waves, lax.axis_index("col"), 0, keepdims=False)
    degree = jnp.arange(degree_count, dtype=jnp.int32)
    bounds = lax.dynamic_index_in_dim(support, band_id, 0, keepdims=False)
    filter_row = lax.dynamic_index_in_dim(band_filter, band_id, 0, keepdims=False)
    window = filter_row * ((degree >= bounds[0]) & (degree < bounds[1])).astype(jnp.float32)

    weights = [
        dft_weights(lat_points, waves[:, c], lon_count)
        for c in range(CHUNKS)
    ]
    outputs = []
    for c in range(CHUNKS):
        fourier = dft(weights[c], grid_field, owners)
        owned = lax.all_to_all(fourier, "col", split_axis=0, concat_axis=0, tiled=True)
        owned = owned.reshape(lat_count, 2, step, owned.shape[3])
        spectral = jnp.einsum(
            "xpsl,sxn->snpl",
            owned,
            lax.slice_in_dim(legendre, c * step, (c + 1) * step, axis=0),
            preferred_element_type=jnp.float32,
        )
        spectral_weight = (degree[None, :] >= owned_waves[c][:, None]).astype(
            jnp.float32
        ) * window[None, :]
        contribution = (spectral * spectral_weight[:, :, None, None]).astype(jnp.bfloat16)
        outputs.append(
            lax.psum_scatter(contribution, "band", scatter_dimension=1, tiled=True)
        )
    return jnp.concatenate(outputs, axis=0).astype(jnp.float32)


def solution(mesh):
    in_specs = (
        P("band", "col", None, None),
        P(),
        P("col", None, None),
        P(),
        P("band", None),
        P(),
        P("col"),
        P(),
    )
    out_specs = P("col", "band", None, None)
    return jax.shard_map(
        per_device, mesh=mesh, in_specs=in_specs, out_specs=out_specs, check_vma=False
    )
```

```python
import math

import jax
import jax.numpy as jnp
from jax import lax
from jax.experimental import pallas as pl
from jax.experimental.pallas import tpu as pltpu
from jax.sharding import PartitionSpec as P

LVR = 112
CHUNKS = (2, 2, 1)


def weights_kernel(points_ref, wave_ref, part_ref, *out_refs):
    count = jnp.full((1, 1), points_ref[pl.program_id(0)], jnp.int32).astype(jnp.float32)
    lons = out_refs[0].shape[2]
    lon = lax.broadcasted_iota(jnp.int32, (1, lons), 1).astype(jnp.float32)
    full = 4.0 * count
    inverse = 1.0 / full
    unit = (2.0 * math.pi) * inverse
    scale = jnp.where(lon < count, lax.rsqrt(count), 0.0)
    nearest = 1.5 * 2.0**23
    first = 0
    for out_ref in out_refs:
        cols = out_ref.shape[1]
        tile = 8 if cols % 16 else 16

        def rows(k, carry, out_ref=out_ref, first=first, tile=tile):
            at = pl.multiple_of(k * tile, tile)
            wave = wave_ref[pl.ds(first + at, tile), :]
            shift = part_ref[pl.ds(first + at, tile), :] * count
            turns = wave * lon + shift
            whole = (turns * inverse + nearest) - nearest
            rest = turns - whole * full
            theta = (count - jnp.abs(rest)) * unit
            square = theta * theta
            value = -1.0 / 39916800.0 * square + 1.0 / 362880.0
            value = value * square - 1.0 / 5040.0
            value = value * square + 1.0 / 120.0
            value = value * square - 1.0 / 6.0
            value = value * square + 1.0
            value = value * (theta * scale)
            out_ref[0, pl.ds(at, tile), :] = value.astype(jnp.bfloat16)
            return carry

        lax.fori_loop(0, cols // tile, rows, 0)
        first += cols


def dft_weights(points, chunks, lon_count):
    lats = points.shape[0]
    wave, part, shapes = [], [], []
    for waves in chunks:
        owners, slots = waves.shape
        shape = (owners, 2, slots)
        wave.append(jnp.broadcast_to(4.0 * waves.astype(jnp.float32)[:, None], shape).reshape(-1))
        part.append(
            jnp.broadcast_to(jnp.arange(2, dtype=jnp.float32)[None, :, None], shape).reshape(-1)
        )
        shapes.append((lats, owners * 2 * slots, lon_count))
    wave = jnp.concatenate(wave)[:, None]
    part = jnp.concatenate(part)[:, None]
    cols = wave.shape[0]
    return pl.pallas_call(
        weights_kernel,
        grid_spec=pltpu.PrefetchScalarGridSpec(
            num_scalar_prefetch=1,
            grid=(lats,),
            in_specs=[pl.BlockSpec((cols, 1), lambda i, p: (0, 0))] * 2,
            out_specs=[pl.BlockSpec((1,) + sh[1:], lambda i, p: (i, 0, 0)) for sh in shapes],
        ),
        out_shape=[jax.ShapeDtypeStruct(sh, jnp.bfloat16) for sh in shapes],
        cost_estimate=pl.CostEstimate(
            flops=25 * lats * cols * lon_count,
            bytes_accessed=2 * lats * cols * lon_count,
            transcendentals=0,
        ),
        name="weights",
    )(points, wave, part)


def dft_kernel(weight_ref, grid_ref, out_ref):
    lons = grid_ref.shape[0] * grid_ref.shape[2]
    owners, _, rows, levels = out_ref.shape
    for i in range(grid_ref.shape[1]):
        column = grid_ref[:, i].reshape(lons, levels)
        result = jnp.dot(weight_ref[i], column, preferred_element_type=jnp.float32)
        out_ref[:, i] = result.astype(jnp.bfloat16).reshape(owners, rows, levels)


def dft(weights, grid_field, owners):
    lats, cols, lons = weights.shape
    ranks, _, lon_local, levels = grid_field.shape
    rows = cols // owners
    block = max(d for d in range(1, 9) if lats % d == 0)
    return pl.pallas_call(
        dft_kernel,
        grid=(lats // block,),
        in_specs=[
            pl.BlockSpec((block, cols, lons), lambda i: (i, 0, 0)),
            pl.BlockSpec((ranks, block, lon_local, levels), lambda i: (0, i, 0, 0)),
        ],
        out_specs=pl.BlockSpec((owners, block, rows, levels), lambda i: (0, i, 0, 0)),
        out_shape=jax.ShapeDtypeStruct((owners, lats, rows, levels), jnp.bfloat16),
        cost_estimate=pl.CostEstimate(
            flops=2 * lats * cols * lons * levels,
            bytes_accessed=2 * lats * (cols * lons + (cols + lons) * levels),
            transcendentals=0,
        ),
        name="dft",
    )(weights, grid_field)


def per_device(
    control, vertical_root, legendre, band_filter, row_plan, wave_order, lat_points, support
):
    owners = lax.axis_size("col")
    band_id = row_plan[0, 0]
    level_start = row_plan[0, 1]
    root_band = lax.dynamic_index_in_dim(vertical_root, band_id, 0, keepdims=False)
    level = jnp.arange(root_band.shape[1], dtype=jnp.int32)
    inside = (level >= level_start) & (level < level_start + LVR)
    root_block = jnp.where(inside[None, :], root_band, jnp.zeros_like(root_band))
    columns = control[0]
    lon_local, lat_count, _ = columns.shape
    rooted = jnp.einsum(
        "jik,kl->ijl", columns, root_block, preferred_element_type=jnp.float32
    ).astype(jnp.bfloat16)
    rooted = rooted.reshape(owners, lat_count // owners, lon_local, -1)
    grid_field = lax.all_to_all(rooted, "col", split_axis=0, concat_axis=0, tiled=True)
    lon_count = lon_local * owners
    lat_local = lat_count // owners

    slot_count = legendre.shape[0]
    degree_count = legendre.shape[2]
    ends = [slot_count * sum(CHUNKS[: c + 1]) // sum(CHUNKS) for c in range(len(CHUNKS))]
    spans = list(zip([0] + ends[:-1], ends))
    waves = wave_order.reshape(owners, slot_count)
    owned_waves = lax.dynamic_index_in_dim(waves, lax.axis_index("col"), 0, keepdims=False)
    degree = jnp.arange(degree_count, dtype=jnp.int32)
    bounds = lax.dynamic_index_in_dim(support, band_id, 0, keepdims=False)
    filter_row = lax.dynamic_index_in_dim(band_filter, band_id, 0, keepdims=False)
    window = filter_row * ((degree >= bounds[0]) & (degree < bounds[1])).astype(jnp.float32)

    weights = dft_weights(lat_points, [waves[:, lo:hi] for lo, hi in spans], lon_count)
    outputs = []
    fourier = dft(weights[0], grid_field, owners)
    for c, (lo, hi) in enumerate(spans):
        owned = lax.all_to_all(fourier, "col", split_axis=0, concat_axis=0, tiled=True)
        if c + 1 < len(spans):
            fourier = dft(weights[c + 1], grid_field, owners)
        if c:
            fourier, owned, _ = lax.optimization_barrier((fourier, owned, contribution))
        else:
            fourier, owned = lax.optimization_barrier((fourier, owned))
        owned = owned.reshape(lat_count, 2, hi - lo, owned.shape[3])
        spectral = jnp.einsum(
            "xpsl,sxn->snpl",
            owned,
            legendre[lo:hi],
            preferred_element_type=jnp.float32,
        )
        spectral_weight = (degree[None, :] >= owned_waves[lo:hi][:, None]).astype(
            jnp.float32
        ) * window[None, :]
        contribution = (spectral * spectral_weight[:, :, None, None]).astype(jnp.bfloat16)
        if c:
            contribution, outputs[-1] = lax.optimization_barrier((contribution, outputs[-1]))
        outputs.append(
            lax.psum_scatter(contribution, "band", scatter_dimension=1, tiled=True)
        )
    return jnp.concatenate(outputs, axis=0).astype(jnp.float32)


def solution(mesh):
    in_specs = (
        P("band", "col", None, None),
        P(),
        P("col", None, None),
        P(),
        P("band", None),
        P(),
        P("col"),
        P(),
    )
    out_specs = P("col", "band", None, None)
    return jax.shard_map(
        per_device, mesh=mesh, in_specs=in_specs, out_specs=out_specs, check_vma=False
    )
```

```python
import math

import jax
import jax.numpy as jnp
from jax import lax
from jax.experimental import pallas as pl
from jax.experimental.pallas import tpu as pltpu
from jax.sharding import PartitionSpec as P

LVR = 112
CHUNKS = (2, 2, 1)


def sine(theta):
    square = theta * theta
    value = -1.0 / 39916800.0 * square + 1.0 / 362880.0
    value = value * square - 1.0 / 5040.0
    value = value * square + 1.0 / 120.0
    value = value * square - 1.0 / 6.0
    value = value * square + 1.0
    return value * theta


def weights_kernel(points_ref, wave_ref, *out_refs):
    count = jnp.full((1, 1), points_ref[pl.program_id(0)], jnp.int32).astype(jnp.float32)
    lons = out_refs[0].shape[2]
    lanes = 128
    lon = lax.broadcasted_iota(jnp.int32, (1, lons), 1).astype(jnp.float32)
    full = 4.0 * count
    inverse = 1.0 / full
    unit = (2.0 * math.pi) * inverse
    scale = jnp.where(lon < count, lax.rsqrt(count), 0.0)
    nearest = 1.5 * 2.0**23
    first = 0
    for out_ref in out_refs:
        half = out_ref.shape[1] // 2
        tile = 8 if half % 16 else 16

        def rows(k, carry, out_ref=out_ref, first=first, tile=tile, half=half):
            at = pl.multiple_of(k * tile, tile)
            turns = wave_ref[pl.ds(first + at, tile), :] * lon[:, :lanes]
            whole = (turns * inverse + nearest) - nearest
            rest = turns - whole * full
            cos = sine((count - jnp.abs(rest)) * unit)
            away = jnp.abs(rest - count)
            sin = sine((count - jnp.minimum(away, full - away)) * unit)
            middle = lanes // 2
            cos_half = jnp.broadcast_to(cos[:, middle : middle + 1], cos.shape)
            sin_half = jnp.broadcast_to(sin[:, middle : middle + 1], sin.shape)
            cos_step = cos_half * cos_half - sin_half * sin_half
            sin_step = 2.0 * (cos_half * sin_half)
            for lo in range(0, lons, lanes):
                if lo:
                    cos, sin = (
                        cos * cos_step - sin * sin_step,
                        sin * cos_step + cos * sin_step,
                    )
                part = scale[:, lo : lo + lanes]
                out_ref[0, pl.ds(at, tile), lo : lo + lanes] = (cos * part).astype(
                    jnp.bfloat16
                )
                out_ref[0, pl.ds(half + at, tile), lo : lo + lanes] = (-sin * part).astype(
                    jnp.bfloat16
                )
            return carry

        lax.fori_loop(0, half // tile, rows, 0)
        first += half


def dft_weights(points, chunks, lon_count):
    lats = points.shape[0]
    shapes = [(lats, 2 * waves.size, lon_count) for waves in chunks]
    wave = jnp.concatenate([waves.reshape(-1) for waves in chunks])
    wave = 4.0 * wave.astype(jnp.float32)[:, None]
    return pl.pallas_call(
        weights_kernel,
        grid_spec=pltpu.PrefetchScalarGridSpec(
            num_scalar_prefetch=1,
            grid=(lats,),
            in_specs=[pl.BlockSpec(wave.shape, lambda i, p: (0, 0))],
            out_specs=[pl.BlockSpec((1,) + sh[1:], lambda i, p: (i, 0, 0)) for sh in shapes],
        ),
        out_shape=[jax.ShapeDtypeStruct(sh, jnp.bfloat16) for sh in shapes],
        cost_estimate=pl.CostEstimate(
            flops=20 * lats * wave.shape[0] * lon_count,
            bytes_accessed=4 * lats * wave.shape[0] * lon_count,
            transcendentals=0,
        ),
        name="weights",
    )(points, wave)


def dft_kernel(weight_ref, grid_ref, out_ref):
    lons = grid_ref.shape[0] * grid_ref.shape[2]
    owners, _, parts, slots, levels = out_ref.shape
    half = owners * slots
    for i in range(grid_ref.shape[1]):
        column = grid_ref[:, i].reshape(lons, levels)
        result = jnp.dot(weight_ref[i], column, preferred_element_type=jnp.float32)
        for p in range(parts):
            piece = result[p * half : (p + 1) * half].reshape(owners, slots, levels)
            out_ref[:, i, p] = piece.astype(jnp.bfloat16)


def dft(weights, grid_field, owners):
    lats, cols, lons = weights.shape
    ranks, _, lon_local, levels = grid_field.shape
    slots = cols // (2 * owners)
    block = max(d for d in range(1, 9) if lats % d == 0)
    return pl.pallas_call(
        dft_kernel,
        grid=(lats // block,),
        in_specs=[
            pl.BlockSpec((block, cols, lons), lambda i: (i, 0, 0)),
            pl.BlockSpec((ranks, block, lon_local, levels), lambda i: (0, i, 0, 0)),
        ],
        out_specs=pl.BlockSpec((owners, block, 2, slots, levels), lambda i: (0, i, 0, 0, 0)),
        out_shape=jax.ShapeDtypeStruct((owners, lats, 2, slots, levels), jnp.bfloat16),
        cost_estimate=pl.CostEstimate(
            flops=2 * lats * cols * lons * levels,
            bytes_accessed=2 * lats * (cols * lons + (cols + lons) * levels),
            transcendentals=0,
        ),
        name="dft",
    )(weights, grid_field)


def per_device(
    control, vertical_root, legendre, band_filter, row_plan, wave_order, lat_points, support
):
    owners = lax.axis_size("col")
    band_id = row_plan[0, 0]
    level_start = row_plan[0, 1]
    root_band = lax.dynamic_index_in_dim(vertical_root, band_id, 0, keepdims=False)
    level = jnp.arange(root_band.shape[1], dtype=jnp.int32)
    inside = (level >= level_start) & (level < level_start + LVR)
    root_block = jnp.where(inside[None, :], root_band, jnp.zeros_like(root_band))
    columns = control[0]
    lon_local, lat_count, _ = columns.shape
    rooted = jnp.einsum(
        "jik,kl->ijl", columns, root_block, preferred_element_type=jnp.float32
    ).astype(jnp.bfloat16)
    rooted = rooted.reshape(owners, lat_count // owners, lon_local, -1)
    grid_field = lax.all_to_all(rooted, "col", split_axis=0, concat_axis=0, tiled=True)
    lon_count = lon_local * owners
    lat_local = lat_count // owners

    slot_count = legendre.shape[0]
    degree_count = legendre.shape[2]
    ends = [slot_count * sum(CHUNKS[: c + 1]) // sum(CHUNKS) for c in range(len(CHUNKS))]
    spans = list(zip([0] + ends[:-1], ends))
    waves = wave_order.reshape(owners, slot_count)
    owned_waves = lax.dynamic_index_in_dim(waves, lax.axis_index("col"), 0, keepdims=False)
    degree = jnp.arange(degree_count, dtype=jnp.int32)
    bounds = lax.dynamic_index_in_dim(support, band_id, 0, keepdims=False)
    filter_row = lax.dynamic_index_in_dim(band_filter, band_id, 0, keepdims=False)
    window = filter_row * ((degree >= bounds[0]) & (degree < bounds[1])).astype(jnp.float32)

    weights = dft_weights(lat_points, [waves[:, lo:hi] for lo, hi in spans], lon_count)
    outputs = []
    fourier = dft(weights[0], grid_field, owners)
    for c, (lo, hi) in enumerate(spans):
        owned = lax.all_to_all(fourier, "col", split_axis=0, concat_axis=0, tiled=True)
        if c + 1 < len(spans):
            fourier = dft(weights[c + 1], grid_field, owners)
        if c:
            fourier, owned, _ = lax.optimization_barrier((fourier, owned, contribution))
        else:
            fourier, owned = lax.optimization_barrier((fourier, owned))
        owned = owned.reshape(lat_count, 2, hi - lo, owned.shape[4])
        spectral = jnp.einsum(
            "xpsl,sxn->snpl",
            owned,
            legendre[lo:hi],
            preferred_element_type=jnp.float32,
        )
        spectral_weight = (degree[None, :] >= owned_waves[lo:hi][:, None]).astype(
            jnp.float32
        ) * window[None, :]
        contribution = (spectral * spectral_weight[:, :, None, None]).astype(jnp.bfloat16)
        if c:
            contribution, outputs[-1] = lax.optimization_barrier((contribution, outputs[-1]))
        outputs.append(
            lax.psum_scatter(contribution, "band", scatter_dimension=1, tiled=True)
        )
    return jnp.concatenate(outputs, axis=0).astype(jnp.float32)


def solution(mesh):
    in_specs = (
        P("band", "col", None, None),
        P(),
        P("col", None, None),
        P(),
        P("band", None),
        P(),
        P("col"),
        P(),
    )
    out_specs = P("col", "band", None, None)
    return jax.shard_map(
        per_device, mesh=mesh, in_specs=in_specs, out_specs=out_specs, check_vma=False
    )
```
